512 devices in a mesh: blk: 16 (over z_lo, x), lab: 32 (over y, z_hi, core).
Axes of the slice: x: 4, y: 8, z: 8 (z_hi: 2, z_lo: 4; z = z_hi * 4 + z_lo), core: 2. Of those that a mesh axis runs over, the one named last changes fastest.
Arguments:
- features: bfloat16 [65536, 768], P(('blk', 'lab')), may hold values from -0.21875 to 0.21875
- direction: bfloat16 [32, 256, 768], P('lab', 'blk'), may hold values from -6 to 6
- active: int32 [65536, 8192], P('blk', 'lab'), may hold values 0 or 1
- shortlist: int32 [512, 64], P('blk', 'lab'), may hold values 0 or 1
Outputs:
- hess_product: float32 [32, 256, 768], P('lab', 'blk')
- curvature: float32 [32, 256], P('lab', 'blk')
The draws below stay inside these ranges and needn't reach their ends.
All inputs are finite; a program needn't handle non-finite values. No bound on the sum of `active` or of `shortlist` on one device may be relied on, other than what follows from the above.
Results may differ from the reference program's by a relative error of at most 0.00059.
Values may be sent and summed in bfloat16 or wider, within the bound.
No kernel may reach another device: no remote copies, remote signals or barrier semaphores. Data moves between devices by JAX's collectives and lax.ppermute only.
A program may use at most 64 MiB of HBM per device.

```python
import jax
import jax.numpy as jnp
from jax import lax

D = 768
TILE = 128
ROWS = 65536
LGROUP = 256
LABELS = 8192
N_LAB = 32


def with_ends(values, key, least, top_value):
    shape = values.shape
    index_at = [jax.random.randint(jax.random.fold_in(key, axis), (), 0, shape[axis]) for axis in range(len(shape))]
    values = values.at[tuple(index_at)].set(least)
    longest = shape.index(max(shape))
    index_at[longest] = (index_at[longest] + 1) % shape[longest]
    return values.at[tuple(index_at)].set(top_value)


def shard_levels(rng, shape, cuts, smallest, top_value):
    level, own = 1.0, jax.random.fold_in(rng, 6)
    for axis_at, parts in cuts:
        draws = jnp.exp(jax.random.uniform(jax.random.fold_in(own, axis_at), (parts,), jnp.float32, smallest / len(cuts), top_value / len(cuts)))
        level = level * jnp.repeat(draws, shape[axis_at] // parts).reshape([-1 if axis == axis_at else 1 for axis in range(len(shape))])
    return level


def scatter_about(own_key, dims, deviation, most, pieces=(), held_as=jnp.bfloat16):
    result = deviation * jax.random.normal(own_key, dims, jnp.float32)
    if pieces:
        result = result * shard_levels(own_key, dims, pieces, -0.22, 0.18)
    return jnp.clip(result, -most, most).astype(held_as)


def setup_inputs(seed: int = 0) -> dict:
    key_list = jax.random.split(jax.random.key(seed), 5)
    features = scatter_about(key_list[0], (ROWS, D), (D ** -0.5), 0.21875, ((0, 512),))
    direction = scatter_about(key_list[1], (N_LAB, LGROUP, D), 1.0, 6.0, ((0, 32), (1, 16)))
    active = with_ends((jax.random.randint(key_list[2], (ROWS, LABELS), 0, 3) < 1).astype(jnp.int32), jax.random.fold_in(key_list[2], 1), 0, 1)
    shortlist = with_ends((jax.random.randint(key_list[3], (ROWS // TILE, LABELS // TILE), 0, 4) < 3).astype(jnp.int32), jax.random.fold_in(key_list[3], 1), 0, 1)
    return dict(features=features, direction=direction, active=active, shortlist=shortlist)


def reference(features, direction, active, shortlist):
    def one_group(group):
        group = group.astype(jnp.int32)
        vectors = direction[group]
        window = lax.dynamic_slice_in_dim(active, (group * LGROUP).astype(jnp.int32), LGROUP, 1)
        tiles = lax.dynamic_slice_in_dim(shortlist, (group * (LGROUP // TILE)).astype(jnp.int32), LGROUP // TILE, 1)
        blocks = window.reshape(ROWS // TILE, TILE, LGROUP // TILE, TILE) * tiles[:, None, :, None]
        weights = blocks.reshape(ROWS, LGROUP).astype(jnp.float32)
        margins = lax.dot_general(features, vectors, (((1,), (1,)), ((), ())), preferred_element_type=jnp.float32)
        scaled = (weights * margins).astype(jnp.bfloat16)
        row_total = lax.dot_general(scaled, features, (((0,), (0,)), ((), ())), preferred_element_type=jnp.float32)
        product = vectors.astype(jnp.float32) + row_total
        curve = jnp.sum(vectors.astype(jnp.float32) * product, axis=-1) / D
        return product, curve

    hess_product, curvature = lax.map(one_group, jnp.arange(N_LAB, dtype=jnp.int32))
    return hess_product, curvature
```

```python
import jax
import jax.numpy as jnp
from jax import lax
from jax.experimental import pallas as pl
from jax.experimental.pallas import tpu as pltpu
from jax.sharding import PartitionSpec as P

D = 768
TILE = 128
N_Y, N_H, N_CORE = 8, 2, 2
N_ZLO, N_X = 4, 4
SUM_SCALE = 4.0


def lab_index(y, h, c):
    return (y % N_Y) * (N_H * N_CORE) + (h % N_H) * N_CORE + c % N_CORE


def lab_perm(target):
    places = [(y, h, c) for y in range(N_Y) for h in range(N_H) for c in range(N_CORE)]
    return [(lab_index(*p), lab_index(*target(*p))) for p in places]


def blk_perm(flip):
    return [(b, b ^ flip) for b in range(N_ZLO * N_X)]


CORE = lab_perm(lambda y, h, c: (y, h, c ^ 1))
ACROSS = lab_perm(lambda y, h, c: (y, h ^ 1, c))
RING = lab_perm(lambda y, h, c: (y + (1 if c == 0 else -1), h, c))
FLIPS = (8, 4, 3, 1)


def owner_flip(place):
    flip = 0
    for bit, step in enumerate(FLIPS):
        if place >> bit & 1:
            flip ^= step
    return flip


def weights_kernel(shortlist_ref, active_ref, out_ref):
    step = pl.program_id(0)
    tiles = active_ref.shape[0] // TILE
    for t in range(tiles):
        for j in range(active_ref.shape[1] // TILE):
            block = active_ref[t * TILE:(t + 1) * TILE, j * TILE:(j + 1) * TILE]
            block = block * shortlist_ref[step * tiles + t, j]
            out_ref[t, j * TILE:(j + 1) * TILE, :] = block.astype(jnp.float32).T.astype(jnp.bfloat16)


def make_weights(active, shortlist):
    rows, labels = active.shape
    per = 512
    return pl.pallas_call(
        weights_kernel,
        grid=(rows // per,),
        in_specs=[
            pl.BlockSpec(memory_space=pltpu.SMEM),
            pl.BlockSpec((per, labels), lambda i: (i, 0)),
        ],
        out_specs=pl.BlockSpec((per // TILE, labels, TILE), lambda i: (i, 0, 0)),
        out_shape=jax.ShapeDtypeStruct((rows // TILE, labels, TILE), jnp.bfloat16),
        compiler_params=pltpu.CompilerParams(vmem_limit_bytes=16 << 20),
        name="make_weights",
    )(shortlist, active)


def sort_kernel(blk_ref, in_ref, out_ref):
    size = in_ref.shape[0] // 16
    for place in range(16):
        start = pl.multiple_of((blk_ref[0] ^ owner_flip(place)) * size, size)
        out_ref[pl.ds(start, size), :] = in_ref[place * size:(place + 1) * size, :]


def sort_blocks(gathered, blk):
    return pl.pallas_call(
        sort_kernel,
        in_specs=[pl.BlockSpec(memory_space=pltpu.SMEM), pl.BlockSpec(memory_space=pltpu.VMEM)],
        out_specs=pl.BlockSpec(memory_space=pltpu.VMEM),
        out_shape=jax.ShapeDtypeStruct(gathered.shape, gathered.dtype),
        compiler_params=pltpu.CompilerParams(vmem_limit_bytes=8 << 20),
        name="sort_blocks",
    )(blk, gathered)


def product_kernel(sizes, places, first, lab_ref, d_own, d_other, w_own, w_other, *refs):
    lab = lab_ref[0]
    y, h, c = lab // (N_H * N_CORE), lab // N_CORE % N_H, lab % N_CORE
    toward = 2 * c - 1
    index = [lab_index(y + N_Y + steps * toward, h + plane, c + core) for steps, plane, core in places]
    chunks = refs[:len(sizes)]
    rest = refs[len(sizes):]
    sums = rest[-2:]
    for group, (d_ref, w_ref) in enumerate(((d_own, w_own), (d_other, w_other))):
        total = None if first else rest[group][...]
        at = 0
        for size, chunk in zip(sizes, chunks):
            blocks = size // TILE
            rows = chunk[...]
            margins = lax.dot_general(
                d_ref[...], rows, (((1,), (1,)), ((), ())), preferred_element_type=jnp.float32
            )
            weights = [w_ref[index[at + k]] for k in range(blocks)]
            weights = weights[0] if blocks == 1 else jnp.concatenate(weights, axis=1)
            scaled = (weights.astype(jnp.float32) * margins).astype(jnp.bfloat16)
            part = jnp.dot(scaled, rows, preferred_element_type=jnp.float32)
            total = part if total is None else total + part
            at += blocks
        sums[group][...] = total


def add_chunks(lab, places, d_own, d_other, w_own, w_other, chunks, before):
    sizes = tuple(c.shape[0] for c in chunks)
    vmem = pl.BlockSpec(memory_space=pltpu.VMEM)
    labels = d_own.shape[0]
    rows = sum(sizes)
    operands = [lab, d_own, d_other, w_own, w_other, *chunks, *(before or ())]
    first = before is None
    aliases = {} if first else {len(operands) - 2: 0, len(operands) - 1: 1}

    def body(*refs):
        product_kernel(sizes, places, first, *refs)

    return pl.pallas_call(
        body,
        in_specs=[pl.BlockSpec(memory_space=pltpu.SMEM)] + [vmem] * (len(operands) - 1),
        out_specs=[vmem, vmem],
        out_shape=[jax.ShapeDtypeStruct((labels, D), jnp.float32)] * 2,
        input_output_aliases=aliases,
        cost_estimate=pl.CostEstimate(
            flops=8 * labels * D * rows, bytes_accessed=4 * labels * D * 4, transcendentals=0
        ),
        compiler_params=pltpu.CompilerParams(vmem_limit_bytes=24 << 20),
        name="add_chunks",
    )(*operands)


def label_scale(vectors):
    return jnp.maximum(jnp.max(jnp.abs(vectors.astype(jnp.float32)), axis=-1, keepdims=True), 1e-30)


def shards(features, direction, active, shortlist):
    vectors = direction[0]
    blk = lax.axis_index("blk").astype(jnp.int32).reshape(1)
    lab = lax.axis_index("lab").astype(jnp.int32).reshape(1)

    def on_lab(value, perm):
        return lax.ppermute(value, "lab", perm)

    beside = on_lab(features, CORE)
    across = on_lab(features, ACROSS)
    near = [jnp.concatenate([features, beside])]
    for k in range(3):
        near.append(on_lab(near[-1], RING))
    near.append(on_lab(near[-1][:TILE], RING))
    far = [jnp.concatenate([across, on_lab(across, CORE)])]
    for k in range(3):
        far.append(on_lab(far[-1], RING))
    far.append(on_lab(far[-1][:TILE], RING))

    gathered = vectors
    for flip in FLIPS:
        gathered = jnp.concatenate([gathered, lax.ppermute(gathered, "blk", blk_perm(flip))])
    d_own = sort_blocks(gathered, blk)
    d_other = on_lab(d_own, CORE)
    w_own = make_weights(active, shortlist)
    w_other = on_lab(w_own, CORE)

    def both(steps, plane):
        return ((steps, plane, 0), (steps, plane, 1))

    def add(chunks, blocks, before):
        return add_chunks(lab, blocks, d_own, d_other, w_own, w_other, chunks, before)

    sums = add([features, near[1], near[2]], ((0, 0, 0), *both(1, 0), *both(2, 0)), None)
    sums = add([across, near[3], far[1]], ((0, 1, 0), *both(3, 0), *both(1, 1)), sums)
    sums = add([near[4], far[2]], ((4, 0, 0), *both(2, 1)), sums)
    own, other = add([far[3], far[4]], (*both(3, 1), (4, 1, 0)), sums)

    slab_sum = own + on_lab(other, CORE)
    sent = (slab_sum * (1.0 / (SUM_SCALE * label_scale(d_own)))).astype(jnp.float16)
    pieces = lax.all_to_all(sent.reshape(16, 16, D), "blk", 0, 0, tiled=True)
    own_total = jnp.sum(pieces.astype(jnp.float32), axis=0) * (SUM_SCALE * label_scale(vectors))
    product = vectors.astype(jnp.float32) + own_total
    curve = jnp.sum(vectors.astype(jnp.float32) * product, axis=-1) / D
    return (product[None], curve[None])


def solution(mesh):
    return jax.shard_map(
        shards,
        mesh=mesh,
        in_specs=(P(("blk", "lab"), None), P("lab", "blk", None), P("blk", "lab"), P("blk", "lab")),
        out_specs=(P("lab", "blk", None), P("lab", "blk")),
        check_vma=False,
    )
```

```python
import jax
import jax.numpy as jnp
from jax import lax
from jax.experimental import pallas as pl
from jax.experimental.pallas import tpu as pltpu
from jax.sharding import PartitionSpec as P


D = 768
TILE = 128
N_Y, N_H, N_CORE = 8, 2, 2
ROW_SCALE = 2.0 ** 17
SUM_SCALE = 4.0


def lab_index(y, h, c):
    return (y * N_H + h) * N_CORE + c


PLACES = [(y, h, c) for y in range(N_Y) for h in range(N_H) for c in range(N_CORE)]
ACROSS = [(lab_index(y, h, c), lab_index(y, 1 - h, c)) for y, h, c in PLACES]
CORE = [(lab_index(y, h, c), lab_index(y, h, 1 - c)) for y, h, c in PLACES]
RINGS = [[lab_index(y, h, c) for y in range(N_Y)] for h in range(N_H) for c in range(N_CORE)]


def weights_kernel(shortlist_ref, active_ref, out_ref):
    step = pl.program_id(0)
    tiles = active_ref.shape[0] // TILE
    for t in range(tiles):
        for j in range(active_ref.shape[1] // TILE):
            block = active_ref[t * TILE:(t + 1) * TILE, j * TILE:(j + 1) * TILE]
            block = block * shortlist_ref[j, step * tiles + t]
            block = block.astype(jnp.float32) * (1.0 / ROW_SCALE)
            out_ref[t, j * TILE:(j + 1) * TILE, :] = block.T.astype(jnp.bfloat16)


def make_weights(active, shortlist):
    rows, labels = active.shape
    per = 512
    return pl.pallas_call(
        weights_kernel,
        grid=(rows // per,),
        in_specs=[
            pl.BlockSpec(memory_space=pltpu.SMEM),
            pl.BlockSpec((per, labels), lambda i: (i, 0)),
        ],
        out_specs=pl.BlockSpec((per // TILE, labels, TILE), lambda i: (i, 0, 0)),
        out_shape=jax.ShapeDtypeStruct((rows // TILE, labels, TILE), jnp.bfloat16),
        compiler_params=pltpu.CompilerParams(vmem_limit_bytes=16 << 20),
        name="make_weights",
    )(shortlist, active)


def product_kernel(first, core_ref, d_ref, w_ref, rows_ref, *refs):
    out_ref = refs[-1]
    pair = N_H * TILE
    for y in range(N_Y):
        rows = rows_ref[y * pair:(y + 1) * pair, :]
        margins = lax.dot_general(
            d_ref[...], rows, (((1,), (1,)), ((), ())), preferred_element_type=jnp.float32
        )
        weights = jnp.concatenate([w_ref[lab_index(y, h, core_ref[0])] for h in range(N_H)], axis=1)
        scaled = (weights.astype(jnp.float32) * margins).astype(jnp.bfloat16)
        part = jnp.dot(scaled, rows, preferred_element_type=jnp.float32)
        if y:
            out_ref[...] += part
        elif first:
            out_ref[...] = part
        else:
            out_ref[...] = refs[0][...] + part


def label_sums(core, gathered, weights, slab, before):
    vmem = pl.BlockSpec(memory_space=pltpu.VMEM)
    first = before is None
    operands = [core, gathered, weights, slab, *([] if first else [before])]

    def body(*refs):
        product_kernel(first, *refs)

    return pl.pallas_call(
        body,
        in_specs=[pl.BlockSpec(memory_space=pltpu.SMEM), *[vmem] * (len(operands) - 1)],
        out_specs=vmem,
        out_shape=jax.ShapeDtypeStruct(gathered.shape, jnp.float32),
        input_output_aliases={} if first else {4: 0},
        cost_estimate=pl.CostEstimate(
            flops=4 * slab.size * gathered.shape[0], bytes_accessed=2 * slab.size, transcendentals=0
        ),
        compiler_params=pltpu.CompilerParams(vmem_limit_bytes=8 << 20),
        name="label_sums",
    )(*operands)


def repeat_kernel(in_ref, out_ref):
    for place in range(out_ref.shape[0]):
        out_ref[place] = in_ref[...]


def repeat(vectors, times):
    vmem = pl.BlockSpec(memory_space=pltpu.VMEM)
    return pl.pallas_call(
        repeat_kernel,
        in_specs=[vmem],
        out_specs=vmem,
        out_shape=jax.ShapeDtypeStruct((times, *vectors.shape), vectors.dtype),
        compiler_params=pltpu.CompilerParams(vmem_limit_bytes=4 << 20),
        name="repeat",
    )(vectors)


def label_scale(vectors):
    return jnp.maximum(jnp.max(jnp.abs(vectors.astype(jnp.float32)), axis=-1, keepdims=True), 1e-30)


def shards(features, direction, active, shortlist):
    return steps(features, direction[0], active, shortlist)


def steps(features, vectors, active, shortlist):
    lab = lax.axis_index("lab")
    h, core = (lab & N_CORE) // N_CORE, (lab & 1).astype(jnp.int32).reshape(1)
    across = lax.ppermute(features, "lab", ACROSS)
    gathered = lax.all_to_all(repeat(vectors, 16), "blk", 0, 0, tiled=True).reshape(-1, D)
    pair = jnp.where(h == 0, jnp.stack([features, across]), jnp.stack([across, features]))
    pair = (pair.astype(jnp.float32) * ROW_SCALE).astype(jnp.float16).reshape(-1, D)
    slab = lax.all_gather(pair, "lab", axis_index_groups=RINGS, axis=0, tiled=True)
    beside = lax.ppermute(slab, "lab", CORE)
    slab, active = lax.optimization_barrier((slab, active))
    weights = make_weights(active, shortlist.T)
    sums = label_sums(core, gathered, weights, slab.astype(jnp.bfloat16), None)
    sums = label_sums(1 - core, gathered, weights, beside.astype(jnp.bfloat16), sums)
    sent = (sums * (1.0 / (SUM_SCALE * ROW_SCALE * label_scale(gathered)))).astype(jnp.float16)
    sent, own_scale = lax.optimization_barrier((sent, SUM_SCALE * label_scale(vectors)))
    pieces = lax.all_to_all(sent.reshape(16, 16, D), "blk", 0, 0, tiled=True)
    own_total = jnp.sum(pieces.astype(jnp.float32), axis=0) * own_scale
    product = vectors.astype(jnp.float32) + own_total
    curve = jnp.sum(vectors.astype(jnp.float32) * product, axis=-1) / D
    return (product[None], curve[None])


def solution(mesh):
    return jax.shard_map(
        shards,
        mesh=mesh,
        in_specs=(P(("blk", "lab"), None), P("lab", "blk", None), P("blk", "lab"), P("blk", "lab")),
        out_specs=(P("lab", "blk", None), P("lab", "blk")),
        check_vma=False,
    )
```

```python
import jax
import jax.numpy as jnp
from jax import lax
from jax.experimental import pallas as pl
from jax.experimental.pallas import tpu as pltpu
from jax.sharding import PartitionSpec as P


D = 768
TILE = 128
N_Y, N_H, N_CORE = 8, 2, 2
ROW_SCALE = 2.0 ** 17
SUM_SCALE = 4.0
VMEM_LIMIT = 48 << 20
N_PARTS = 4
STOPS = (0, 2, 5, 8)


def lab_index(y, h, c):
    return (y * N_H + h) * N_CORE + c


PLACES = [(y, h, c) for y in range(N_Y) for h in range(N_H) for c in range(N_CORE)]
ACROSS = [(lab_index(y, h, c), lab_index(y, 1 - h, c)) for y, h, c in PLACES]
CORE = [(lab_index(y, h, c), lab_index(y, h, 1 - c)) for y, h, c in PLACES]
RINGS = [[lab_index(y, h, c) for y in range(N_Y)] for h in range(N_H) for c in range(N_CORE)]


def weights_kernel(shortlist_ref, active_hbm, out_ref, active_ref, arrived):
    tiles, labels = active_ref.shape[0] // TILE, active_ref.shape[1]
    per = tiles // N_PARTS

    def fetch(part):
        rows = pl.ds(part * per * TILE, per * TILE)
        return pltpu.make_async_copy(active_hbm.at[rows, :], active_ref.at[rows, :], arrived.at[part])

    for part in range(N_PARTS):
        fetch(part).start()
    for t in range(tiles):
        if t % per == 0:
            fetch(t // per).wait()
        for j in range(labels // TILE):
            block = active_ref[t * TILE:(t + 1) * TILE, j * TILE:(j + 1) * TILE]
            block = (block * shortlist_ref[j, t]).astype(jnp.float32) * (1.0 / ROW_SCALE)
            out_ref[t, j * TILE:(j + 1) * TILE, :] = block.T.astype(jnp.bfloat16)


def make_weights(active, shortlist):
    rows, labels = active.shape
    return pl.pallas_call(
        weights_kernel,
        in_specs=[pl.BlockSpec(memory_space=pltpu.SMEM), pl.BlockSpec(memory_space=pl.ANY)],
        out_specs=pl.BlockSpec(memory_space=pltpu.VMEM),
        out_shape=jax.ShapeDtypeStruct((rows // TILE, labels, TILE), jnp.bfloat16),
        scratch_shapes=[pltpu.VMEM(active.shape, jnp.int32), pltpu.SemaphoreType.DMA((N_PARTS,))],
        compiler_params=pltpu.CompilerParams(vmem_limit_bytes=VMEM_LIMIT),
        name="make_weights",
    )(shortlist, active)


def product_kernel(first, core_ref, d_ref, w_ref, rows_hbm, *refs):
    before, (out_ref, rows_ref, arrived) = refs[:-3], refs[-3:]
    pair = N_H * TILE

    def fetch(part):
        rows = pl.ds(STOPS[part] * pair, (STOPS[part + 1] - STOPS[part]) * pair)
        return pltpu.make_async_copy(rows_hbm.at[rows, :], rows_ref.at[rows, :], arrived.at[part])

    for part in range(len(STOPS) - 1):
        fetch(part).start()
    for y in range(N_Y):
        if y in STOPS:
            fetch(STOPS.index(y)).wait()
        rows = rows_ref[y * pair:(y + 1) * pair, :]
        margins = lax.dot_general(
            d_ref[...], rows, (((1,), (1,)), ((), ())), preferred_element_type=jnp.float32
        )
        weights = jnp.concatenate([w_ref[lab_index(y, h, core_ref[0])] for h in range(N_H)], axis=1)
        scaled = (weights.astype(jnp.float32) * margins).astype(jnp.bfloat16)
        part = jnp.dot(scaled, rows, preferred_element_type=jnp.float32)
        if y:
            out_ref[...] += part
        elif first:
            out_ref[...] = part
        else:
            out_ref[...] = before[0][...] + part


def label_sums(core, gathered, weights, slab, before):
    vmem = pl.BlockSpec(memory_space=pltpu.VMEM)
    first = before is None
    operands = [core, gathered, weights, slab, *([] if first else [before])]

    def body(*refs):
        product_kernel(first, *refs)

    return pl.pallas_call(
        body,
        in_specs=[
            pl.BlockSpec(memory_space=pltpu.SMEM), vmem, vmem, pl.BlockSpec(memory_space=pl.ANY),
            *([] if first else [vmem]),
        ],
        out_specs=vmem,
        out_shape=jax.ShapeDtypeStruct(gathered.shape, jnp.float32),
        scratch_shapes=[
            pltpu.VMEM(slab.shape, jnp.bfloat16), pltpu.SemaphoreType.DMA((len(STOPS) - 1,)),
        ],
        input_output_aliases={} if first else {4: 0},
        cost_estimate=pl.CostEstimate(
            flops=4 * slab.size * gathered.shape[0], bytes_accessed=2 * slab.size, transcendentals=0
        ),
        compiler_params=pltpu.CompilerParams(vmem_limit_bytes=VMEM_LIMIT),
        name="label_sums",
    )(*operands)


def repeat_kernel(in_ref, out_ref):
    for place in range(out_ref.shape[0]):
        out_ref[place] = in_ref[...]


def repeat(vectors, times):
    vmem = pl.BlockSpec(memory_space=pltpu.VMEM)
    return pl.pallas_call(
        repeat_kernel,
        in_specs=[vmem],
        out_specs=vmem,
        out_shape=jax.ShapeDtypeStruct((times, *vectors.shape), vectors.dtype),
        compiler_params=pltpu.CompilerParams(vmem_limit_bytes=4 << 20),
        name="repeat",
    )(vectors)


def label_scale(vectors):
    return jnp.maximum(jnp.max(jnp.abs(vectors.astype(jnp.float32)), axis=-1, keepdims=True), 1e-30)


def shards(features, direction, active, shortlist):
    return steps(features, direction[0], active, shortlist)


def steps(features, vectors, active, shortlist):
    lab = lax.axis_index("lab")
    h, core = (lab & N_CORE) // N_CORE, (lab & 1).astype(jnp.int32).reshape(1)
    across = lax.ppermute(features, "lab", ACROSS)
    gathered = lax.all_to_all(repeat(vectors, 16), "blk", 0, 0, tiled=True).reshape(-1, D)
    pair = jnp.where(h == 0, jnp.stack([features, across]), jnp.stack([across, features]))
    pair = (pair.astype(jnp.float32) * ROW_SCALE).astype(jnp.float16).reshape(-1, D)
    slab = lax.all_gather(pair, "lab", axis_index_groups=RINGS, axis=0, tiled=True)
    slab = slab.astype(jnp.bfloat16)
    beside = lax.ppermute(slab, "lab", CORE)
    weights = make_weights(active, shortlist.T)
    sums = label_sums(core, gathered, weights, slab, None)
    sums = label_sums(1 - core, gathered, weights, beside, sums)
    sent = (sums * (1.0 / (SUM_SCALE * ROW_SCALE * label_scale(gathered)))).astype(jnp.float16)
    sent, own_scale = lax.optimization_barrier((sent, SUM_SCALE * label_scale(vectors)))
    pieces = lax.all_to_all(sent.reshape(16, 16, D), "blk", 0, 0, tiled=True)
    own_total = jnp.sum(pieces.astype(jnp.float32), axis=0) * own_scale
    product = vectors.astype(jnp.float32) + own_total
    curve = jnp.sum(vectors.astype(jnp.float32) * product, axis=-1) / D
    return (product[None], curve[None])


def solution(mesh):
    return jax.shard_map(
        shards,
        mesh=mesh,
        in_specs=(P(("blk", "lab"), None), P("lab", "blk", None), P("blk", "lab"), P("blk", "lab")),
        out_specs=(P("lab", "blk", None), P("lab", "blk")),
        check_vma=False,
    )
```

```python
import jax
import jax.numpy as jnp
from jax import lax
from jax.experimental import pallas as pl
from jax.experimental.pallas import tpu as pltpu
from jax.sharding import PartitionSpec as P


D = 768
TILE = 128
N_Y, N_H, N_CORE = 8, 2, 2
ROW_SCALE = 2.0 ** 17
SUM_SCALE = 4.0
VMEM_LIMIT = 48 << 20
N_PARTS = 4
STOPS = (0, 1, 4, 8)


def lab_index(y, h, c):
    return (y * N_H + h) * N_CORE + c


PLACES = [(y, h, c) for y in range(N_Y) for h in range(N_H) for c in range(N_CORE)]
ACROSS = [(lab_index(y, h, c), lab_index(y, 1 - h, c)) for y, h, c in PLACES]
CORE = [(lab_index(y, h, c), lab_index(y, h, 1 - c)) for y, h, c in PLACES]
RINGS = [[lab_index(y, h, c) for y in range(N_Y)] for h in range(N_H) for c in range(N_CORE)]


def add_rows(core, d_ref, w_ref, rows_ref, before_ref, out_ref, arrive):
    pair = N_H * TILE
    for y in range(N_Y):
        if y in STOPS:
            arrive(STOPS.index(y)).wait()
        rows = rows_ref[y * pair:(y + 1) * pair, :]
        margins = lax.dot_general(
            d_ref[...], rows, (((1,), (1,)), ((), ())), preferred_element_type=jnp.float32
        )
        weights = jnp.concatenate([w_ref[lab_index(y, h, core)] for h in range(N_H)], axis=1)
        scaled = (weights.astype(jnp.float32) * margins).astype(jnp.bfloat16)
        part = jnp.dot(scaled, rows, preferred_element_type=jnp.float32)
        if y:
            out_ref[...] += part
        elif before_ref is None:
            out_ref[...] = part
        else:
            out_ref[...] = before_ref[...] + part


def fetch_rows(rows_hbm, rows_ref, rows_in, part):
    pair = N_H * TILE
    rows = pl.ds(STOPS[part] * pair, (STOPS[part + 1] - STOPS[part]) * pair)
    return pltpu.make_async_copy(rows_hbm.at[rows, :], rows_ref.at[rows, :], rows_in.at[part])


def own_kernel(
    core_ref, shortlist_ref, d_ref, active_hbm, rows_hbm, w_ref, out_ref, active_ref, rows_ref, active_in, rows_in
):
    tiles, labels = active_ref.shape[0] // TILE, active_ref.shape[1]
    per = tiles // N_PARTS

    def fetch_active(part):
        rows = pl.ds(part * per * TILE, per * TILE)
        return pltpu.make_async_copy(active_hbm.at[rows, :], active_ref.at[rows, :], active_in.at[part])

    def arrive(part):
        return fetch_rows(rows_hbm, rows_ref, rows_in, part)

    for part in range(N_PARTS):
        fetch_active(part).start()
    for part in range(len(STOPS) - 1):
        arrive(part).start()
    for t in range(tiles):
        if t % per == 0:
            fetch_active(t // per).wait()
        for j in range(labels // TILE):
            block = active_ref[t * TILE:(t + 1) * TILE, j * TILE:(j + 1) * TILE]
            block = (block * shortlist_ref[j, t]).astype(jnp.float32) * (1.0 / ROW_SCALE)
            w_ref[t, j * TILE:(j + 1) * TILE, :] = block.T.astype(jnp.bfloat16)
    add_rows(core_ref[0], d_ref, w_ref, rows_ref, None, out_ref, arrive)


def other_kernel(core_ref, d_ref, w_ref, rows_hbm, before_ref, out_ref, rows_ref, rows_in):
    def arrive(part):
        return fetch_rows(rows_hbm, rows_ref, rows_in, part)

    for part in range(len(STOPS) - 1):
        arrive(part).start()
    add_rows(core_ref[0], d_ref, w_ref, rows_ref, before_ref, out_ref, arrive)


SMEM, VMEM = pl.BlockSpec(memory_space=pltpu.SMEM), pl.BlockSpec(memory_space=pltpu.VMEM)
IN_PLACE = pl.BlockSpec(memory_space=pl.ANY)


def cost_of(slab, gathered):
    return pl.CostEstimate(
        flops=4 * slab.size * gathered.shape[0], bytes_accessed=2 * slab.size, transcendentals=0
    )


def own_sums(core, shortlist, gathered, active, slab):
    rows, labels = active.shape
    return pl.pallas_call(
        own_kernel,
        in_specs=[SMEM, SMEM, VMEM, IN_PLACE, IN_PLACE],
        out_specs=[VMEM, VMEM],
        out_shape=[
            jax.ShapeDtypeStruct((rows // TILE, labels, TILE), jnp.bfloat16),
            jax.ShapeDtypeStruct(gathered.shape, jnp.float32),
        ],
        scratch_shapes=[
            pltpu.VMEM(active.shape, jnp.int32),
            pltpu.VMEM(slab.shape, jnp.bfloat16),
            pltpu.SemaphoreType.DMA((N_PARTS,)),
            pltpu.SemaphoreType.DMA((len(STOPS) - 1,)),
        ],
        cost_estimate=cost_of(slab, gathered),
        compiler_params=pltpu.CompilerParams(vmem_limit_bytes=VMEM_LIMIT),
        name="own_sums",
    )(core, shortlist, gathered, active, slab)


def add_other(core, gathered, weights, slab, before):
    return pl.pallas_call(
        other_kernel,
        in_specs=[SMEM, VMEM, VMEM, IN_PLACE, VMEM],
        out_specs=VMEM,
        out_shape=jax.ShapeDtypeStruct(gathered.shape, jnp.float32),
        scratch_shapes=[
            pltpu.VMEM(slab.shape, jnp.bfloat16), pltpu.SemaphoreType.DMA((len(STOPS) - 1,)),
        ],
        input_output_aliases={4: 0},
        cost_estimate=cost_of(slab, gathered),
        compiler_params=pltpu.CompilerParams(vmem_limit_bytes=VMEM_LIMIT),
        name="add_other",
    )(core, gathered, weights, slab, before)


def repeat_kernel(in_ref, out_ref):
    for place in range(out_ref.shape[0]):
        out_ref[place] = in_ref[...]


def repeat(vectors, times):
    vmem = pl.BlockSpec(memory_space=pltpu.VMEM)
    return pl.pallas_call(
        repeat_kernel,
        in_specs=[vmem],
        out_specs=vmem,
        out_shape=jax.ShapeDtypeStruct((times, *vectors.shape), vectors.dtype),
        compiler_params=pltpu.CompilerParams(vmem_limit_bytes=4 << 20),
        name="repeat",
    )(vectors)


def label_scale(vectors):
    return jnp.maximum(jnp.max(jnp.abs(vectors.astype(jnp.float32)), axis=-1, keepdims=True), 1e-30)


def shards(features, direction, active, shortlist):
    return steps(features, direction[0], active, shortlist)


def steps(features, vectors, active, shortlist):
    lab = lax.axis_index("lab")
    h, core = (lab & N_CORE) // N_CORE, (lab & 1).astype(jnp.int32).reshape(1)
    across = lax.ppermute(features, "lab", ACROSS)
    gathered = lax.all_to_all(repeat(vectors, 16), "blk", 0, 0, tiled=True).reshape(-1, D)
    pair = jnp.where(h == 0, jnp.stack([features, across]), jnp.stack([across, features]))
    pair = (pair.astype(jnp.float32) * ROW_SCALE).astype(jnp.float16).reshape(-1, D)
    slab = lax.all_gather(pair, "lab", axis_index_groups=RINGS, axis=0, tiled=True)
    slab = slab.astype(jnp.bfloat16)
    beside = lax.ppermute(slab, "lab", CORE)
    weights, sums = own_sums(core, shortlist.T, gathered, active, slab)
    sums = add_other(1 - core, gathered, weights, beside, sums)
    sent = (sums * (1.0 / (SUM_SCALE * ROW_SCALE * label_scale(gathered)))).astype(jnp.float16)
    sent, own_scale = lax.optimization_barrier((sent, SUM_SCALE * label_scale(vectors)))
    pieces = lax.all_to_all(sent.reshape(16, 16, D), "blk", 0, 0, tiled=True)
    own_total = jnp.sum(pieces.astype(jnp.float32), axis=0) * own_scale
    product = vectors.astype(jnp.float32) + own_total
    curve = jnp.sum(vectors.astype(jnp.float32) * product, axis=-1) / D
    return (product[None], curve[None])


def solution(mesh):
    return jax.shard_map(
        shards,
        mesh=mesh,
        in_specs=(P(("blk", "lab"), None), P("lab", "blk", None), P("blk", "lab"), P("blk", "lab")),
        out_specs=(P("lab", "blk", None), P("lab", "blk")),
        check_vma=False,
    )
```
